512 devices in a mesh: grp: 32 (over y_hi, x, core), row: 16 (over y_lo, z).
Axes of the slice: x: 4, y: 8 (y_hi: 4, y_lo: 2; y = y_hi * 2 + y_lo), z: 8, core: 2. Of those that a mesh axis runs over, the one named last changes fastest.
Arguments:
- starter: float32 [2, 256, 256, 512], P(None, 'grp', 'row'), may hold values from -6 to 6
- medium: float32 [256, 512], P('row'), may hold values from -0.5 to 0.5
- csm: float32 [2, 256, 256], replicated, as said below
- capon_weight: float32 [2, 256, 256], replicated, as said below
- search_cells: int32 [16, 8192], P('row'), may hold values from 0 to 8191, each once within a row
Outputs:
- bartlett_power: float32 [16, 8192], P('row', 'grp')
- capon_power: float32 [16, 8192], P('row', 'grp')
The draws below stay inside these ranges and needn't reach their ends.
Inputs may be any that keep to these rules, and one draw needn't show every extreme that they name: `search_cells`: each row is a permutation of the 8192 cells of its slab. csm[0] + i csm[1] is Hermitian and positive definite. capon_weight[0] + i capon_weight[1] is Hermitian and positive definite.
All inputs are finite; a program needn't handle non-finite values.
Results may differ from the reference program's by a relative error of at most 0.00005.
Values sent between devices are 32-bit elements; how exact they have to be, the bound alone decides.
A program may use at most 64 MiB of HBM per device.

```python
import jax
import jax.numpy as jnp
from jax import lax

H = 256
RW = 16
CROSS = 512
STEPS = 2
ROWS = 256
N_ROW = 16


def hermitian_draw(key):
    keys = jax.random.split(key, 4)
    upper_real = jnp.triu(jax.random.uniform(keys[0], (H, H), jnp.float32, -1.0, 1.0), 1) / H
    upper_imag = jnp.triu(jax.random.uniform(keys[1], (H, H), jnp.float32, -1.0, 1.0), 1) / H
    base = 1.5 + 0.5 * jax.random.uniform(keys[2], (H,), jnp.float32)
    scales = jnp.exp(jax.random.uniform(keys[3], (H,), jnp.float32, -0.2, 0.2))
    outer = scales[:, None] * scales[None, :]
    real_part = (upper_real + upper_real.T + jnp.diag(base)) * outer
    imag_part = (upper_imag - upper_imag.T) * outer
    return jnp.stack([real_part, imag_part], axis=0)


def draw_csm(key, part):
    return hermitian_draw(jax.random.fold_in(key, 11))


def draw_capon_weight(key, part):
    return hermitian_draw(jax.random.fold_in(key, 23))


def levels(own_key, extent, pieces, smallest, largest):
    loudness, own = 1.0, jax.random.fold_in(own_key, 6)
    for dim, parts in pieces:
        draws = jnp.exp(jax.random.uniform(jax.random.fold_in(own, dim), (parts,), jnp.float32, smallest / len(pieces), largest / len(pieces)))
        loudness = loudness * jnp.repeat(draws, extent[dim] // parts).reshape([-1 if axis == dim else 1 for axis in range(len(extent))])
    return loudness


def centred(own_key, extent, deviation, bound, pieces=(), kind=jnp.bfloat16):
    values = jax.random.normal(own_key, extent, jnp.float32) * deviation
    if len(pieces) > 0:
        values = levels(own_key, extent, pieces, -0.22, 0.18) * values
    return jnp.clip(values, min=-bound, max=bound).astype(kind)


def setup_inputs(seed: int = 0) -> dict:
    streams_of = jax.random.split(jax.random.key(seed), 6)
    return {
        "starter": centred(streams_of[0], (2, H, ROWS, CROSS), 1.0, 6.0, ((1, 32), (2, 16)), jnp.float32),
        "medium": jnp.clip(jax.random.uniform(streams_of[1], (ROWS, CROSS), jnp.float32, -0.5, 0.5) * levels(streams_of[1], (ROWS, CROSS), ((0, 16),), -0.4, 0.0), -0.5, 0.5),
        "csm": draw_csm(jax.random.fold_in(streams_of[5], 71), 0),
        "capon_weight": draw_capon_weight(jax.random.fold_in(streams_of[5], 71), 0),
        "search_cells": jax.vmap(lambda own: jax.random.permutation(own, RW * CROSS))(jax.random.split(streams_of[4], N_ROW)).reshape((N_ROW, RW * CROSS)).astype(jnp.int32),
    }


lap_scale = 0.5
first_coef = (0.0, 0.25)
second_coef = (-0.03, -0.02)


def combine(coef, values):
    real_part = coef[0] * values[0] - coef[1] * values[1]
    imag_part = coef[1] * values[0] + coef[0] * values[1]
    return jnp.stack([real_part, imag_part], axis=0)


def operate(field, medium):
    padded = jnp.pad(field, ((0, 0), (1, 1), (1, 1)))
    laplace = padded[:, 2:, 1:-1] + padded[:, :-2, 1:-1] + padded[:, 1:-1, 2:] + padded[:, 1:-1, :-2] - 4.0 * field
    return lap_scale * laplace + medium * field


def real_form(matrix):
    real_part = matrix[0]
    imag_part = matrix[1]
    return jnp.concatenate([jnp.concatenate([real_part, -imag_part], axis=1), jnp.concatenate([imag_part, real_part], axis=1)], axis=0)


def reference(starter, medium, csm, capon_weight, search_cells):
    def one_replica(index):
        field = starter[:, index]
        for marching in range(STEPS):
            first_pass = operate(field, medium)
            second_pass = operate(first_pass, medium)
            field = field + combine(first_coef, first_pass) + combine(second_coef, second_pass)
        return field

    replicas = lax.map(one_replica, jnp.arange(H, dtype=jnp.int32))
    slabs = replicas.reshape(H, 2, N_ROW, RW * CROSS)
    embed = real_form(csm)
    weighting = real_form(capon_weight)

    def slab_surfaces(index):
        data = slabs[:, :, index]
        picked = jnp.take(data, search_cells[index], axis=2)
        vectors = jnp.transpose(picked, (1, 0, 2)).reshape(2 * H, RW * CROSS)
        power = jnp.sum(vectors * vectors, axis=0) + 1e-6
        bartlett = jnp.sum(vectors * jnp.dot(embed, vectors, precision=lax.Precision.HIGHEST), axis=0) / power
        capon = power / jnp.sum(vectors * jnp.dot(weighting, vectors, precision=lax.Precision.HIGHEST), axis=0)
        return jnp.stack([bartlett, capon], axis=0)

    result = lax.map(slab_surfaces, jnp.arange(N_ROW, dtype=jnp.int32))
    return result[:, 0], result[:, 1]
```

```python
import jax
import jax.numpy as jnp
from jax import lax
from jax.sharding import PartitionSpec as P

STEPS = 2
RIM = 2 * STEPS

lap_scale = 0.5
first_coef = (0.0, 0.25)
second_coef = (-0.03, -0.02)


def with_rim(cells, axis):
    count = lax.axis_size(axis)
    rows = cells.shape[1]
    above = lax.ppermute(cells[:, rows - RIM :], axis, [(i, i + 1) for i in range(count - 1)])
    below = lax.ppermute(cells[:, :RIM], axis, [(i + 1, i) for i in range(count - 1)])
    return jnp.concatenate([above, cells, below], axis=1)


def apply_operator(field, medium, inside):
    padded = jnp.pad(field, ((0, 0), (1, 1), (1, 1)))
    laplace = (
        padded[:, 2:, 1:-1]
        + padded[:, :-2, 1:-1]
        + padded[:, 1:-1, 2:]
        + padded[:, 1:-1, :-2]
        - 4.0 * field
    )
    return jnp.where(inside, lap_scale * laplace + medium * field, 0.0)


def march(field, first_pass, second_pass):
    half = field.shape[0] // 2
    fr, fi = first_pass[:half], first_pass[half:]
    sr, si = second_pass[:half], second_pass[half:]
    real = field[:half] + (first_coef[0] * fr - first_coef[1] * fi) + (second_coef[0] * sr - second_coef[1] * si)
    imag = field[half:] + (first_coef[1] * fr + first_coef[0] * fi) + (second_coef[1] * sr + second_coef[0] * si)
    return jnp.concatenate([real, imag], axis=0)


def form(matrix, u, v):
    def dot(a, b):
        return jnp.dot(a, b, precision=lax.Precision.HIGHEST)

    both = dot(matrix[0], jnp.concatenate([u, v], axis=1))
    cells = u.shape[1]
    cross = dot(matrix[1], u)
    return jnp.sum(u * both[:, :cells] + v * both[:, cells:] + 2.0 * (v * cross), axis=0)


def on_device(starter, medium, csm, capon_weight, search_cells):
    parts, hydros, slab_rows, cross_cells = starter.shape
    planes = parts * hydros
    packed = jnp.concatenate([starter.reshape(planes, slab_rows, cross_cells), medium[None]], axis=0)
    packed = with_rim(packed, "row")
    field, medium = packed[:planes], packed[planes]
    depth = lax.axis_index("row") * slab_rows - RIM + lax.broadcasted_iota(jnp.int32, medium.shape, 0)
    inside = (depth >= 0) & (depth < lax.axis_size("row") * slab_rows)
    for marching in range(STEPS):
        first_pass = apply_operator(field, medium, inside)
        second_pass = apply_operator(first_pass, medium, inside)
        field = march(field, first_pass, second_pass)
    field = field[:, RIM : RIM + slab_rows]
    owners = lax.axis_size("grp")
    pieces = field.reshape(parts, hydros, owners, -1)
    vectors = lax.all_to_all(pieces, "grp", split_axis=2, concat_axis=1, tiled=True)[:, :, 0]
    u, v = vectors[0], vectors[1]
    power = jnp.sum(u * u + v * v, axis=0) + 1e-06
    bartlett = form(csm, u, v) / power
    capon = power / form(capon_weight, u, v)
    mine = jnp.stack([bartlett, capon], axis=0)
    cells = mine.shape[1]
    copies = jnp.broadcast_to(mine[None], (owners, 2, cells))
    table = lax.all_to_all(copies, "grp", split_axis=0, concat_axis=0, tiled=True)
    table = jnp.swapaxes(table, 0, 1).reshape(2, owners * cells)
    wanted = lax.dynamic_slice(search_cells, (0, lax.axis_index("grp") * cells), (1, cells))[0]
    result = jnp.take(table, wanted, axis=1)
    return (result[0][None, :], result[1][None, :])


def solution(mesh):
    return jax.shard_map(
        on_device,
        mesh=mesh,
        in_specs=(P(None, "grp", "row", None), P("row", None), P(), P(), P("row", None)),
        out_specs=(P("row", "grp"), P("row", "grp")),
        check_vma=False,
    )
```

```python
import functools

import jax
import jax.numpy as jnp
from jax import lax
from jax.experimental import pallas as pl
from jax.experimental.pallas import tpu as pltpu
from jax.sharding import PartitionSpec as P

STEPS = 2
RIM = 2 * STEPS
LANES = 128
MESH = pl.DeviceIdType.MESH

first_imag = 0.25
second_coef = (-0.03, -0.02)


def kernel(
    owners, slabs, rows,
    starter_ref, medium_ref, csm_ref, weight_ref, cells_ref,
    bartlett_ref, capon_ref,
    start, field, first, middle, coef, medium_above, medium_below,
    outgoing, vectors, csm, weight, mine, table,
    start_sem, local_sem, rim_send, rim_recv, block_send, block_recv, result_send, result_recv,
):
    me = lax.axis_index("grp")
    slab = lax.axis_index("row")
    above = lax.rem(slab + slabs - 1, slabs)
    below = lax.rem(slab + 1, slabs)
    hydros, cols = field.shape[2:]
    tiles = cols // LANES
    inner = rows // 2

    barrier = pltpu.get_barrier_semaphore()
    for other in (above, below):
        pl.semaphore_signal(barrier, inc=1, device_id={"row": other}, device_id_type=MESH)

    @pl.loop(1, owners)
    def _(step):
        other = lax.rem(me + step, owners)
        pl.semaphore_signal(barrier, inc=1, device_id={"grp": other}, device_id_type=MESH)

    loads = []
    for t in range(tiles):
        load = pltpu.make_async_copy(
            starter_ref.at[:, :, t * LANES : (t + 1) * LANES], start.at[t], start_sem.at[t]
        )
        load.start()
        loads.append(load)
    load_csm = pltpu.make_async_copy(csm_ref, csm, local_sem.at[1])
    load_csm.start()
    load_weight = pltpu.make_async_copy(weight_ref, weight, local_sem.at[2])
    load_weight.start()

    def spread(ref, r):
        return jnp.broadcast_to(ref[r : r + 1, :], (hydros, cols)) - 2.0

    for r in range(rows):
        coef[RIM + r] = spread(medium_ref, r)
    for t in range(tiles):
        loads[t].wait()
        for part in range(2):
            for r in range(rows):
                field[part, RIM + r, :, t * LANES : (t + 1) * LANES] = start[
                    t, part, pl.ds(r, hydros, stride=rows), :
                ]

    col = lax.broadcasted_iota(jnp.int32, (hydros, cols), 1)

    def operate(ref, part, r, half):
        here = ref[part, r]
        left = jnp.where(col == 0, 0.0, pltpu.roll(here, 1, 1))
        right = jnp.where(col == cols - 1, 0.0, pltpu.roll(here, cols - 1, 1))
        total = (ref[part, r - 1] + ref[part, r + 1]) + (left + right)
        return half * total + coef[r] * here

    def scale(r):
        outside = ((slab == 0) & (r < RIM)) | ((slab == slabs - 1) & (r >= RIM + rows))
        return jnp.where(outside, 0.0, 0.5).astype(jnp.float32)

    def apply_first(source, r):
        half = scale(r)
        for part in range(2):
            first[part, r] = operate(source, part, r, half)

    def advance(source, r):
        half = scale(r)
        fr, fi = first[0, r], first[1, r]
        sr = operate(first, 0, r, half)
        si = operate(first, 1, r, half)
        real = source[0, r] - first_imag * fi + second_coef[0] * sr - second_coef[1] * si
        imag = source[1, r] + first_imag * fr + second_coef[1] * sr + second_coef[0] * si
        return real, imag

    def first_one(r):
        apply_first(field, r)

    def step_one(r):
        real, imag = advance(field, r)
        middle[0, r] = real
        middle[1, r] = imag

    def first_two(r):
        apply_first(middle, r)

    def step_two(block, base, r):
        real, imag = advance(middle, r)
        for t in range(tiles):
            owner = (r - base) * tiles + t
            outgoing[block, owner, 0] = real[:, t * LANES : (t + 1) * LANES]
            outgoing[block, owner, 1] = imag[:, t * LANES : (t + 1) * LANES]

    def loop(low, high, body):
        lax.fori_loop(low, high, lambda r, c: (body(r), c)[1], 0)

    loop(RIM + 1, RIM + rows - 1, first_one)
    loop(RIM + 2, RIM + rows - 2, step_one)
    loop(RIM + 3, RIM + rows - 3, first_two)
    loop(RIM + 4, RIM + rows - 4, functools.partial(step_two, 0, RIM + 4))

    pl.semaphore_wait(barrier, owners + 1)

    def rim_copy(k, source, target, other):
        return pltpu.make_async_remote_copy(
            src_ref=source, dst_ref=target, send_sem=rim_send.at[k], recv_sem=rim_recv.at[k],
            device_id={"row": other}, device_id_type=MESH,
        )

    rims = [
        rim_copy(0, field.at[:, pl.ds(RIM, RIM)], field.at[:, pl.ds(RIM + rows, RIM)], above),
        rim_copy(1, field.at[:, pl.ds(rows, RIM)], field.at[:, pl.ds(0, RIM)], below),
        rim_copy(2, medium_ref.at[pl.ds(0, 8)], medium_below, above),
        rim_copy(3, medium_ref.at[pl.ds(rows - 8, 8)], medium_above, below),
    ]
    for copy in rims:
        copy.start()

    def block_copy(block, source, target):
        return pltpu.make_async_remote_copy(
            src_ref=outgoing.at[block, target], dst_ref=vectors.at[block, source],
            send_sem=block_send.at[block, target], recv_sem=block_recv.at[block, source],
            device_id={"grp": target}, device_id_type=MESH,
        )

    def send_blocks(block):
        @pl.loop(1, owners)
        def _(step):
            block_copy(block, me, lax.rem(me + step, owners)).start()

        own = pltpu.make_async_copy(
            outgoing.at[block, me], vectors.at[block, me], local_sem.at[3 + block]
        )
        own.start()
        return own

    own_inner = send_blocks(0)

    for copy in rims:
        copy.wait_recv()

    @pl.when(slab == 0)
    def _():
        field[:, 0:RIM] = jnp.zeros((2, RIM, hydros, cols), jnp.float32)

    @pl.when(slab == slabs - 1)
    def _():
        field[:, RIM + rows :] = jnp.zeros((2, RIM, hydros, cols), jnp.float32)

    for r in range(RIM):
        coef[r] = spread(medium_above, 8 - RIM + r)
        coef[RIM + rows + r] = spread(medium_below, r)

    top = RIM + rows
    loop(1, 5, first_one)
    loop(top - 1, top + 3, first_one)
    loop(2, 6, step_one)
    loop(top - 2, top + 2, step_one)
    loop(3, 7, first_two)
    loop(top - 3, top + 1, first_two)
    loop(4, 8, functools.partial(step_two, 1, RIM))
    loop(top - 4, top, functools.partial(step_two, 1, RIM + inner))

    own_outer = send_blocks(1)

    load_csm.wait()
    load_weight.wait()
    own_inner.wait()
    own_outer.wait()
    for block in range(2):
        @pl.loop(1, owners)
        def _(step):
            block_copy(block, lax.rem(me + step, owners), me).wait_recv()

    def stacked(part):
        return jnp.concatenate(
            [vectors[block, :, part].reshape(owners * hydros, LANES) for block in range(2)], axis=1
        )

    u, v = stacked(0), stacked(1)
    power = jnp.sum(u * u + v * v, axis=0, keepdims=True) + 1e-06

    def form(matrix):
        def dot(a, b):
            return jnp.dot(
                a, b, precision=lax.Precision.HIGHEST, preferred_element_type=jnp.float32
            )

        return jnp.sum(
            u * dot(matrix[0], u) + v * (dot(matrix[0], v) + 2.0 * dot(matrix[1], u)),
            axis=0, keepdims=True,
        )

    bartlett = form(csm) / power
    capon = power / form(weight)
    mine[0:1] = bartlett[:, :LANES]
    mine[1:2] = bartlett[:, LANES:]
    mine[2:3] = capon[:, :LANES]
    mine[3:4] = capon[:, LANES:]

    def result_copy(source, target):
        return pltpu.make_async_remote_copy(
            src_ref=mine, dst_ref=table.at[source],
            send_sem=result_send.at[target], recv_sem=result_recv.at[source],
            device_id={"grp": target}, device_id_type=MESH,
        )

    @pl.loop(1, owners)
    def _(step):
        result_copy(me, lax.rem(me + step, owners)).start()

    own_result = pltpu.make_async_copy(mine, table.at[me], local_sem.at[5])
    own_result.start()

    share = bartlett_ref.shape[1]
    wanted = cells_ref[:, pl.ds(pl.multiple_of(me * share, share), share)]
    tile = wanted // LANES
    lane = wanted - tile * LANES
    edge = (inner // 2) * tiles
    is_inner = (tile >= edge) & (tile < edge + owners)
    owner = jnp.where(is_inner, tile - edge, jnp.where(tile < edge, tile, tile - owners))
    entry = owner * 4 + jnp.where(is_inner, 0, 1)
    place = lax.broadcasted_iota(jnp.int32, (owners * 4, share), 0)
    pick_bartlett = jnp.where(place == entry, 1.0, 0.0)
    pick_capon = jnp.where(place == entry + 2, 1.0, 0.0)
    on_lane = lax.broadcasted_iota(jnp.int32, (LANES, share), 0) == lane

    own_result.wait()

    @pl.loop(1, owners)
    def _(step):
        result_copy(lax.rem(me + step, owners), me).wait_recv()

    flat = table[...].reshape(owners * 4, LANES).T

    def take(pick):
        chosen = jnp.dot(
            flat, pick, precision=lax.Precision.HIGHEST, preferred_element_type=jnp.float32
        )
        return jnp.sum(jnp.where(on_lane, chosen, 0.0), axis=0, keepdims=True)

    bartlett_ref[...] = take(pick_bartlett)
    capon_ref[...] = take(pick_capon)

    for copy in rims:
        copy.wait_send()

    @pl.loop(1, owners)
    def _(step):
        other = lax.rem(me + step, owners)
        block_copy(0, me, other).wait_send()
        block_copy(1, me, other).wait_send()
        result_copy(me, other).wait_send()


def on_device(starter, medium, csm, capon_weight, search_cells):
    parts, hydros, rows, cols = starter.shape
    owners = lax.axis_size("grp")
    slabs = lax.axis_size("row")
    depth = rows + 2 * RIM
    share = search_cells.shape[1] // owners
    vmem = pl.BlockSpec(memory_space=pltpu.VMEM)
    anywhere = pl.BlockSpec(memory_space=pl.ANY)
    plane = pltpu.VMEM((parts, depth, hydros, cols), jnp.float32)
    blocks = pltpu.VMEM((2, owners, parts, hydros, LANES), jnp.float32)
    return pl.pallas_call(
        functools.partial(kernel, owners, slabs, rows),
        out_shape=[jax.ShapeDtypeStruct((1, share), jnp.float32)] * 2,
        in_specs=[anywhere, vmem, anywhere, anywhere, vmem],
        out_specs=[vmem, vmem],
        scratch_shapes=[
            pltpu.VMEM((cols // LANES, parts, hydros * rows, LANES), jnp.float32),
            plane,
            plane,
            plane,
            pltpu.VMEM((depth, hydros, cols), jnp.float32),
            pltpu.VMEM((8, cols), jnp.float32),
            pltpu.VMEM((8, cols), jnp.float32),
            blocks,
            blocks,
            pltpu.VMEM(csm.shape, jnp.float32),
            pltpu.VMEM(csm.shape, jnp.float32),
            pltpu.VMEM((4, LANES), jnp.float32),
            pltpu.VMEM((owners, 4, LANES), jnp.float32),
            pltpu.SemaphoreType.DMA((cols // LANES,)),
            pltpu.SemaphoreType.DMA((6,)),
            pltpu.SemaphoreType.DMA((4,)),
            pltpu.SemaphoreType.DMA((4,)),
            pltpu.SemaphoreType.DMA((2, owners)),
            pltpu.SemaphoreType.DMA((2, owners)),
            pltpu.SemaphoreType.DMA((owners,)),
            pltpu.SemaphoreType.DMA((owners,)),
        ],
        compiler_params=pltpu.CompilerParams(collective_id=0, has_side_effects=True),
    )(starter.reshape(parts, hydros * rows, cols), medium, csm, capon_weight, search_cells)


def solution(mesh):
    return jax.shard_map(
        on_device,
        mesh=mesh,
        in_specs=(P(None, "grp", "row", None), P("row", None), P(), P(), P("row", None)),
        out_specs=(P("row", "grp"), P("row", "grp")),
        check_vma=False,
    )
```

```python
import functools

import jax
import jax.numpy as jnp
from jax import lax
from jax.experimental import pallas as pl
from jax.experimental.pallas import tpu as pltpu
from jax.sharding import PartitionSpec as P

STEPS = 2
RIM = 2 * STEPS
LANES = 128
MESH = pl.DeviceIdType.MESH

first_imag = 0.25
second_coef = (-0.03, -0.02)


def kernel(
    owners, slabs, rows,
    starter_ref, medium_ref, csm_ref, weight_ref, cells_ref,
    result_ref,
    start, field, first, middle, coef, medium_above, medium_below,
    outgoing, vectors, csm, weight, mine, table,
    start_sem, local_sem, rim_send, rim_recv, block_send, block_recv, result_send, result_recv,
):
    me = lax.axis_index("grp")
    slab = lax.axis_index("row")
    above = lax.rem(slab + slabs - 1, slabs)
    below = lax.rem(slab + 1, slabs)
    hydros, cols = field.shape[2:]
    tiles = cols // LANES
    inner = rows // 2

    barrier = pltpu.get_barrier_semaphore()
    for other in (above, below):
        pl.semaphore_signal(barrier, inc=1, device_id={"row": other}, device_id_type=MESH)

    @pl.loop(1, owners)
    def _(step):
        other = lax.rem(me + step, owners)
        pl.semaphore_signal(barrier, inc=1, device_id={"grp": other}, device_id_type=MESH)

    loads = []
    for t in range(tiles):
        load = pltpu.make_async_copy(
            starter_ref.at[:, :, t * LANES : (t + 1) * LANES], start.at[t], start_sem.at[t]
        )
        load.start()
        loads.append(load)
    load_csm = pltpu.make_async_copy(csm_ref, csm, local_sem.at[1])
    load_weight = pltpu.make_async_copy(weight_ref, weight, local_sem.at[2])

    def spread(ref, r):
        return jnp.broadcast_to(ref[r : r + 1, :], (hydros, cols)) - 2.0

    def place_rows(which):
        for t in range(tiles):
            for part in range(2):
                for r in which:
                    field[part, RIM + r, :, t * LANES : (t + 1) * LANES] = start[
                        t, part, pl.ds(r, hydros, stride=rows), :
                    ]

    for load in loads:
        load.wait()
    place_rows([*range(RIM), *range(rows - RIM, rows)])

    col = lax.broadcasted_iota(jnp.int32, (hydros, cols), 1)

    def operate(ref, part, r, half):
        here = ref[part, r]
        left = jnp.where(col == 0, 0.0, pltpu.roll(here, 1, 1))
        right = jnp.where(col == cols - 1, 0.0, pltpu.roll(here, cols - 1, 1))
        total = (ref[part, r - 1] + ref[part, r + 1]) + (left + right)
        return half * total + coef[r] * here

    def scale(r):
        if not isinstance(r, int) or RIM <= r < RIM + rows:
            return 0.5
        outside = slab == (0 if r < RIM else slabs - 1)
        return jnp.where(outside, 0.0, 0.5).astype(jnp.float32)

    def apply_first(source, r):
        half = scale(r)
        for part in range(2):
            first[part, r] = operate(source, part, r, half)

    def advance(source, r):
        half = scale(r)
        fr, fi = first[0, r], first[1, r]
        sr = operate(first, 0, r, half)
        si = operate(first, 1, r, half)
        real = source[0, r] - first_imag * fi + second_coef[0] * sr - second_coef[1] * si
        imag = source[1, r] + first_imag * fr + second_coef[1] * sr + second_coef[0] * si
        return real, imag

    def first_one(r):
        apply_first(field, r)

    def step_one(r):
        real, imag = advance(field, r)
        middle[0, r] = real
        middle[1, r] = imag

    def first_two(r):
        apply_first(middle, r)

    def step_two(block, base, r):
        real, imag = advance(middle, r)
        for t in range(tiles):
            owner = (r - base) * tiles + t
            outgoing[block, owner, 0] = real[:, t * LANES : (t + 1) * LANES]
            outgoing[block, owner, 1] = imag[:, t * LANES : (t + 1) * LANES]

    pl.semaphore_wait(barrier, owners + 1)

    def rim_copy(k, source, target, other):
        return pltpu.make_async_remote_copy(
            src_ref=source, dst_ref=target, send_sem=rim_send.at[k], recv_sem=rim_recv.at[k],
            device_id={"row": other}, device_id_type=MESH,
        )

    rims = [
        rim_copy(0, field.at[:, pl.ds(RIM, RIM)], field.at[:, pl.ds(RIM + rows, RIM)], above),
        rim_copy(1, field.at[:, pl.ds(rows, RIM)], field.at[:, pl.ds(0, RIM)], below),
        rim_copy(2, medium_ref.at[pl.ds(0, 8)], medium_below, above),
        rim_copy(3, medium_ref.at[pl.ds(rows - 8, 8)], medium_above, below),
    ]
    for copy in rims:
        copy.start()

    def block_copy(block, source, target):
        return pltpu.make_async_remote_copy(
            src_ref=outgoing.at[block, target], dst_ref=vectors.at[block, source],
            send_sem=block_send.at[block, target], recv_sem=block_recv.at[block, source],
            device_id={"grp": target}, device_id_type=MESH,
        )

    def send_blocks(block):
        @pl.loop(1, owners)
        def _(step):
            block_copy(block, me, lax.rem(me + step, owners)).start()

        own = pltpu.make_async_copy(
            outgoing.at[block, me], vectors.at[block, me], local_sem.at[3 + block]
        )
        own.start()
        return own

    load_csm.start()
    load_weight.start()
    place_rows(range(RIM, rows - RIM))
    for r in range(rows):
        coef[RIM + r] = spread(medium_ref, r)

    def pairs(low, high, body):
        def both(i, carry):
            body(low + 2 * i)
            body(low + 2 * i + 1)
            return carry

        lax.fori_loop(0, (high - low) // 2, both, 0)

    pairs(RIM + 1, RIM + rows - 1, first_one)
    pairs(RIM + 2, RIM + rows - 2, step_one)
    pairs(RIM + 3, RIM + rows - 3, first_two)
    pairs(RIM + 4, RIM + rows - 4, functools.partial(step_two, 0, RIM + 4))

    own_inner = send_blocks(0)

    for copy in rims:
        copy.wait_recv()

    @pl.when(slab == 0)
    def _():
        field[:, 0:RIM] = jnp.zeros((2, RIM, hydros, cols), jnp.float32)

    @pl.when(slab == slabs - 1)
    def _():
        field[:, RIM + rows :] = jnp.zeros((2, RIM, hydros, cols), jnp.float32)

    for r in range(RIM):
        coef[r] = spread(medium_above, 8 - RIM + r)
        coef[RIM + rows + r] = spread(medium_below, r)

    top = RIM + rows
    for stage, body in enumerate((first_one, step_one, first_two)):
        for r in range(RIM):
            body(1 + stage + r)
            body(top - 1 - stage + r)
    for r in range(RIM):
        step_two(1, RIM, RIM + r)
        step_two(1, RIM + inner, top - RIM + r)

    own_outer = send_blocks(1)

    load_csm.wait()
    load_weight.wait()
    own_inner.wait()
    own_outer.wait()
    for block in range(2):
        @pl.loop(1, owners)
        def _(step):
            block_copy(block, lax.rem(me + step, owners), me).wait_recv()

    def stacked(part):
        return jnp.concatenate(
            [vectors[block, :, part].reshape(owners * hydros, LANES) for block in range(2)], axis=1
        )

    u, v = stacked(0), stacked(1)
    power = jnp.sum(u * u + v * v, axis=0, keepdims=True) + 1e-06

    def form(matrix):
        def dot(a, b):
            return jnp.dot(
                a, b, precision=lax.Precision.HIGHEST, preferred_element_type=jnp.float32
            )

        return jnp.sum(
            u * dot(matrix[0], u) + v * (dot(matrix[0], v) + 2.0 * dot(matrix[1], u)),
            axis=0, keepdims=True,
        )

    bartlett = form(csm) / power
    capon = power / form(weight)
    mine[0:1] = bartlett[:, :LANES]
    mine[1:2] = bartlett[:, LANES:]
    mine[2:3] = capon[:, :LANES]
    mine[3:4] = capon[:, LANES:]

    def result_copy(source, target):
        return pltpu.make_async_remote_copy(
            src_ref=mine, dst_ref=table.at[source],
            send_sem=result_send.at[target], recv_sem=result_recv.at[source],
            device_id={"grp": target}, device_id_type=MESH,
        )

    @pl.loop(1, owners)
    def _(step):
        result_copy(me, lax.rem(me + step, owners)).start()

    own_result = pltpu.make_async_copy(mine, table.at[me], local_sem.at[5])
    own_result.start()

    share = result_ref.shape[1]
    wanted = cells_ref[:, pl.ds(pl.multiple_of(me * share, share), share)]
    tile = wanted // LANES
    lane = wanted - tile * LANES
    edge = (inner // 2) * tiles
    is_inner = (tile >= edge) & (tile < edge + owners)
    owner = jnp.where(is_inner, tile - edge, jnp.where(tile < edge, tile, tile - owners))
    entry = owner * 4 + jnp.where(is_inner, 0, 1)
    place = lax.broadcasted_iota(jnp.int32, (owners * 4, share), 0)
    pick_bartlett = jnp.where(place == entry, 1.0, 0.0)
    pick_capon = jnp.where(place == entry + 2, 1.0, 0.0)
    on_lane = lax.broadcasted_iota(jnp.int32, (LANES, share), 0) == lane

    own_result.wait()

    @pl.loop(1, owners)
    def _(step):
        result_copy(lax.rem(me + step, owners), me).wait_recv()

    flat = table[...].reshape(owners * 4, LANES).T

    def take(pick):
        chosen = jnp.dot(
            flat, pick, precision=lax.Precision.HIGHEST, preferred_element_type=jnp.float32
        )
        return jnp.sum(jnp.where(on_lane, chosen, 0.0), axis=0, keepdims=True)

    result_ref[0:1] = take(pick_bartlett)
    result_ref[1:2] = take(pick_capon)

    for copy in rims:
        copy.wait_send()

    @pl.loop(1, owners)
    def _(step):
        other = lax.rem(me + step, owners)
        block_copy(0, me, other).wait_send()
        block_copy(1, me, other).wait_send()
        result_copy(me, other).wait_send()


def on_device(starter, medium, csm, capon_weight, search_cells):
    parts, hydros, rows, cols = starter.shape
    owners = lax.axis_size("grp")
    slabs = lax.axis_size("row")
    depth = rows + 2 * RIM
    share = search_cells.shape[1] // owners
    vmem = pl.BlockSpec(memory_space=pltpu.VMEM)
    anywhere = pl.BlockSpec(memory_space=pl.ANY)
    plane = pltpu.VMEM((parts, depth, hydros, cols), jnp.float32)
    blocks = pltpu.VMEM((2, owners, parts, hydros, LANES), jnp.float32)
    result = pl.pallas_call(
        functools.partial(kernel, owners, slabs, rows),
        out_shape=jax.ShapeDtypeStruct((2, share), jnp.float32),
        in_specs=[anywhere, vmem, anywhere, anywhere, vmem],
        out_specs=vmem,
        scratch_shapes=[
            pltpu.VMEM((cols // LANES, parts, hydros * rows, LANES), jnp.float32),
            plane,
            plane,
            plane,
            pltpu.VMEM((depth, hydros, cols), jnp.float32),
            pltpu.VMEM((8, cols), jnp.float32),
            pltpu.VMEM((8, cols), jnp.float32),
            blocks,
            blocks,
            pltpu.VMEM(csm.shape, jnp.float32),
            pltpu.VMEM(csm.shape, jnp.float32),
            pltpu.VMEM((4, LANES), jnp.float32),
            pltpu.VMEM((owners, 4, LANES), jnp.float32),
            pltpu.SemaphoreType.DMA((cols // LANES,)),
            pltpu.SemaphoreType.DMA((6,)),
            pltpu.SemaphoreType.DMA((4,)),
            pltpu.SemaphoreType.DMA((4,)),
            pltpu.SemaphoreType.DMA((2, owners)),
            pltpu.SemaphoreType.DMA((2, owners)),
            pltpu.SemaphoreType.DMA((owners,)),
            pltpu.SemaphoreType.DMA((owners,)),
        ],
        compiler_params=pltpu.CompilerParams(collective_id=0, has_side_effects=True),
    )(starter.reshape(parts, hydros * rows, cols), medium, csm, capon_weight, search_cells)
    return result[0:1], result[1:2]


def solution(mesh):
    return jax.shard_map(
        on_device,
        mesh=mesh,
        in_specs=(P(None, "grp", "row", None), P("row", None), P(), P(), P("row", None)),
        out_specs=(P("row", "grp"), P("row", "grp")),
        check_vma=False,
    )
```

```python
import functools

import jax
import jax.numpy as jnp
from jax import lax
from jax.experimental import pallas as pl
from jax.experimental.pallas import tpu as pltpu
from jax.sharding import PartitionSpec as P

STEPS = 2
RIM = 2 * STEPS
LANES = 128
MESH = pl.DeviceIdType.MESH

first_imag = 0.25
second_coef = (-0.03, -0.02)


def kernel(
    owners, slabs, rows,
    starter_ref, medium_ref, csm_ref, weight_ref, cells_ref,
    result_ref,
    start, field, first, middle, coef, medium_above, medium_below,
    outgoing, vectors, csm, weight, mine, table,
    start_sem, local_sem, rim_send, rim_recv, block_send, block_recv, result_send, result_recv,
):
    me = lax.axis_index("grp")
    slab = lax.axis_index("row")
    above = lax.rem(slab + slabs - 1, slabs)
    below = lax.rem(slab + 1, slabs)
    hydros, cols = field.shape[2:]
    tiles = cols // LANES
    inner = rows // 2

    def farthest_first(step):
        odd = lax.rem(step, 2)
        return lax.rem(
            me + owners // 2 + odd * (step // 2) + (1 - odd) * (owners - step // 2), owners
        )

    barrier = pltpu.get_barrier_semaphore()
    for other in (above, below):
        pl.semaphore_signal(barrier, inc=1, device_id={"row": other}, device_id_type=MESH)

    @pl.loop(1, owners)
    def _(step):
        other = lax.rem(me + step, owners)
        pl.semaphore_signal(barrier, inc=1, device_id={"grp": other}, device_id_type=MESH)

    loads = []
    for t in range(tiles):
        load = pltpu.make_async_copy(
            starter_ref.at[:, :, t * LANES : (t + 1) * LANES], start.at[t], start_sem.at[t]
        )
        load.start()
        loads.append(load)
    load_csm = pltpu.make_async_copy(csm_ref, csm, local_sem.at[1])
    load_weight = pltpu.make_async_copy(weight_ref, weight, local_sem.at[2])

    def spread(ref, r):
        return jnp.broadcast_to(ref[r : r + 1, :], (hydros, cols)) - 2.0

    def place_rows(which):
        for t in range(tiles):
            for part in range(2):
                for r in which:
                    field[part, RIM + r, :, t * LANES : (t + 1) * LANES] = start[
                        t, part, pl.ds(r, hydros, stride=rows), :
                    ]

    for load in loads:
        load.wait()
    place_rows([*range(RIM), *range(rows - RIM, rows)])

    col = lax.broadcasted_iota(jnp.int32, (hydros, cols), 1)

    def operate(ref, part, r, half):
        here = ref[part, r]
        left = jnp.where(col == 0, 0.0, pltpu.roll(here, 1, 1))
        right = jnp.where(col == cols - 1, 0.0, pltpu.roll(here, cols - 1, 1))
        total = (ref[part, r - 1] + ref[part, r + 1]) + (left + right)
        return half * total + coef[r] * here

    def scale(r):
        if not isinstance(r, int) or RIM <= r < RIM + rows:
            return 0.5
        outside = slab == (0 if r < RIM else slabs - 1)
        return jnp.where(outside, 0.0, 0.5).astype(jnp.float32)

    def apply_first(source, r):
        half = scale(r)
        for part in range(2):
            first[part, r] = operate(source, part, r, half)

    def advance(source, r):
        half = scale(r)
        fr, fi = first[0, r], first[1, r]
        sr = operate(first, 0, r, half)
        si = operate(first, 1, r, half)
        real = source[0, r] - first_imag * fi + second_coef[0] * sr - second_coef[1] * si
        imag = source[1, r] + first_imag * fr + second_coef[1] * sr + second_coef[0] * si
        return real, imag

    def first_one(r):
        apply_first(field, r)

    def step_one(r):
        real, imag = advance(field, r)
        middle[0, r] = real
        middle[1, r] = imag

    def first_two(r):
        apply_first(middle, r)

    def step_two(block, base, r):
        real, imag = advance(middle, r)
        for t in range(tiles):
            owner = (r - base) * tiles + t
            outgoing[block, owner, 0] = real[:, t * LANES : (t + 1) * LANES]
            outgoing[block, owner, 1] = imag[:, t * LANES : (t + 1) * LANES]

    pl.semaphore_wait(barrier, owners + 1)

    def rim_copy(k, source, target, other):
        return pltpu.make_async_remote_copy(
            src_ref=source, dst_ref=target, send_sem=rim_send.at[k], recv_sem=rim_recv.at[k],
            device_id={"row": other}, device_id_type=MESH,
        )

    rims = [
        rim_copy(0, field.at[:, pl.ds(RIM, RIM)], field.at[:, pl.ds(RIM + rows, RIM)], above),
        rim_copy(1, field.at[:, pl.ds(rows, RIM)], field.at[:, pl.ds(0, RIM)], below),
        rim_copy(2, medium_ref.at[pl.ds(0, 8)], medium_below, above),
        rim_copy(3, medium_ref.at[pl.ds(rows - 8, 8)], medium_above, below),
    ]
    for copy in rims:
        copy.start()

    def block_copy(block, source, target):
        return pltpu.make_async_remote_copy(
            src_ref=outgoing.at[block, target], dst_ref=vectors.at[block, source],
            send_sem=block_send.at[block, target], recv_sem=block_recv.at[block, source],
            device_id={"grp": target}, device_id_type=MESH,
        )

    def send_blocks(block):
        @pl.loop(1, owners)
        def _(step):
            block_copy(block, me, farthest_first(step)).start()

        own = pltpu.make_async_copy(
            outgoing.at[block, me], vectors.at[block, me], local_sem.at[3 + block]
        )
        own.start()
        return own

    load_csm.start()
    load_weight.start()
    place_rows(range(RIM, rows - RIM))
    for r in range(rows):
        coef[RIM + r] = spread(medium_ref, r)

    def pairs(low, high, body):
        def both(i, carry):
            body(low + 2 * i)
            body(low + 2 * i + 1)
            return carry

        lax.fori_loop(0, (high - low) // 2, both, 0)

    pairs(RIM + 1, RIM + rows - 1, first_one)
    pairs(RIM + 2, RIM + rows - 2, step_one)
    pairs(RIM + 3, RIM + rows - 3, first_two)
    pairs(RIM + 4, RIM + rows - 4, functools.partial(step_two, 0, RIM + 4))

    own_inner = send_blocks(0)

    for copy in rims:
        copy.wait_recv()

    @pl.when(slab == 0)
    def _():
        field[:, 0:RIM] = jnp.zeros((2, RIM, hydros, cols), jnp.float32)

    @pl.when(slab == slabs - 1)
    def _():
        field[:, RIM + rows :] = jnp.zeros((2, RIM, hydros, cols), jnp.float32)

    for r in range(RIM):
        coef[r] = spread(medium_above, 8 - RIM + r)
        coef[RIM + rows + r] = spread(medium_below, r)

    top = RIM + rows
    for stage, body in enumerate((first_one, step_one, first_two)):
        for r in range(RIM):
            body(1 + stage + r)
            body(top - 1 - stage + r)
    for r in range(RIM):
        step_two(1, RIM, RIM + r)
        step_two(1, RIM + inner, top - RIM + r)

    own_outer = send_blocks(1)

    load_csm.wait()
    load_weight.wait()
    own_inner.wait()
    own_outer.wait()
    for block in range(2):
        @pl.loop(1, owners)
        def _(step):
            block_copy(block, lax.rem(me + step, owners), me).wait_recv()

    def stacked(part):
        return jnp.concatenate(
            [vectors[block, :, part].reshape(owners * hydros, LANES) for block in range(2)], axis=1
        )

    u, v = stacked(0), stacked(1)
    power = jnp.sum(u * u + v * v, axis=0, keepdims=True) + 1e-06

    def form(matrix):
        def dot(a, b):
            return jnp.dot(
                a, b, precision=lax.Precision.HIGHEST, preferred_element_type=jnp.float32
            )

        return jnp.sum(
            u * dot(matrix[0], u) + v * (dot(matrix[0], v) + 2.0 * dot(matrix[1], u)),
            axis=0, keepdims=True,
        )

    bartlett = form(csm) / power
    capon = power / form(weight)
    mine[0:1] = bartlett[:, :LANES]
    mine[1:2] = bartlett[:, LANES:]
    mine[2:3] = capon[:, :LANES]
    mine[3:4] = capon[:, LANES:]

    def result_copy(source, target):
        return pltpu.make_async_remote_copy(
            src_ref=mine, dst_ref=table.at[source],
            send_sem=result_send.at[target], recv_sem=result_recv.at[source],
            device_id={"grp": target}, device_id_type=MESH,
        )

    @pl.loop(1, owners)
    def _(step):
        result_copy(me, farthest_first(step)).start()

    own_result = pltpu.make_async_copy(mine, table.at[me], local_sem.at[5])
    own_result.start()

    share = result_ref.shape[1]
    wanted = cells_ref[:, pl.ds(pl.multiple_of(me * share, share), share)]
    tile = wanted // LANES
    lane = wanted - tile * LANES
    edge = (inner // 2) * tiles
    is_inner = (tile >= edge) & (tile < edge + owners)
    owner = jnp.where(is_inner, tile - edge, jnp.where(tile < edge, tile, tile - owners))
    entry = owner * 4 + jnp.where(is_inner, 0, 1)
    place = lax.broadcasted_iota(jnp.int32, (owners * 4, share), 0)
    pick_bartlett = jnp.where(place == entry, 1.0, 0.0)
    pick_capon = jnp.where(place == entry + 2, 1.0, 0.0)
    on_lane = lax.broadcasted_iota(jnp.int32, (LANES, share), 0) == lane

    own_result.wait()

    @pl.loop(1, owners)
    def _(step):
        result_copy(lax.rem(me + step, owners), me).wait_recv()

    flat = table[...].reshape(owners * 4, LANES).T

    def take(pick):
        chosen = jnp.dot(
            flat, pick, precision=lax.Precision.HIGHEST, preferred_element_type=jnp.float32
        )
        return jnp.sum(jnp.where(on_lane, chosen, 0.0), axis=0, keepdims=True)

    result_ref[0:1] = take(pick_bartlett)
    result_ref[1:2] = take(pick_capon)

    for copy in rims:
        copy.wait_send()

    @pl.loop(1, owners)
    def _(step):
        other = lax.rem(me + step, owners)
        block_copy(0, me, other).wait_send()
        block_copy(1, me, other).wait_send()
        result_copy(me, other).wait_send()


def on_device(starter, medium, csm, capon_weight, search_cells):
    parts, hydros, rows, cols = starter.shape
    owners = lax.axis_size("grp")
    slabs = lax.axis_size("row")
    depth = rows + 2 * RIM
    share = search_cells.shape[1] // owners
    vmem = pl.BlockSpec(memory_space=pltpu.VMEM)
    anywhere = pl.BlockSpec(memory_space=pl.ANY)
    plane = pltpu.VMEM((parts, depth, hydros, cols), jnp.float32)
    blocks = pltpu.VMEM((2, owners, parts, hydros, LANES), jnp.float32)
    result = pl.pallas_call(
        functools.partial(kernel, owners, slabs, rows),
        out_shape=jax.ShapeDtypeStruct((2, share), jnp.float32),
        in_specs=[anywhere, vmem, anywhere, anywhere, vmem],
        out_specs=vmem,
        scratch_shapes=[
            pltpu.VMEM((cols // LANES, parts, hydros * rows, LANES), jnp.float32),
            plane,
            plane,
            plane,
            pltpu.VMEM((depth, hydros, cols), jnp.float32),
            pltpu.VMEM((8, cols), jnp.float32),
            pltpu.VMEM((8, cols), jnp.float32),
            blocks,
            blocks,
            pltpu.VMEM(csm.shape, jnp.float32),
            pltpu.VMEM(csm.shape, jnp.float32),
            pltpu.VMEM((4, LANES), jnp.float32),
            pltpu.VMEM((owners, 4, LANES), jnp.float32),
            pltpu.SemaphoreType.DMA((cols // LANES,)),
            pltpu.SemaphoreType.DMA((6,)),
            pltpu.SemaphoreType.DMA((4,)),
            pltpu.SemaphoreType.DMA((4,)),
            pltpu.SemaphoreType.DMA((2, owners)),
            pltpu.SemaphoreType.DMA((2, owners)),
            pltpu.SemaphoreType.DMA((owners,)),
            pltpu.SemaphoreType.DMA((owners,)),
        ],
        compiler_params=pltpu.CompilerParams(collective_id=0, has_side_effects=True),
    )(starter.reshape(parts, hydros * rows, cols), medium, csm, capon_weight, search_cells)
    return result[0:1], result[1:2]


def solution(mesh):
    return jax.shard_map(
        on_device,
        mesh=mesh,
        in_specs=(P(None, "grp", "row", None), P("row", None), P(), P(), P("row", None)),
        out_specs=(P("row", "grp"), P("row", "grp")),
        check_vma=False,
    )
```

```python
import functools

import jax
import jax.numpy as jnp
from jax import lax
from jax.experimental import pallas as pl
from jax.experimental.pallas import tpu as pltpu
from jax.sharding import PartitionSpec as P

STEPS = 2
RIM = 2 * STEPS
LANES = 128
MESH = pl.DeviceIdType.MESH

first_imag = 0.25
second_coef = (-0.03, -0.02)


def kernel(
    owners, slabs, rows,
    starter_ref, medium_ref, csm_ref, weight_ref, cells_ref,
    result_ref,
    start, field, first, middle, coef, medium_above, medium_below,
    outgoing, vectors, csm, weight, mine, table,
    start_sem, local_sem, rim_send, rim_recv, block_send, block_recv, result_send, result_recv,
):
    me = lax.axis_index("grp")
    slab = lax.axis_index("row")
    above = lax.rem(slab + slabs - 1, slabs)
    below = lax.rem(slab + 1, slabs)
    hydros, cols = field.shape[2:]
    tiles = cols // LANES
    inner = rows // 2

    def farthest_first(step):
        odd = lax.rem(step, 2)
        return lax.rem(
            me + owners // 2 + odd * (step // 2) + (1 - odd) * (owners - step // 2), owners
        )

    barrier = pltpu.get_barrier_semaphore()
    for other in (above, below):
        pl.semaphore_signal(barrier, inc=1, device_id={"row": other}, device_id_type=MESH)

    @pl.loop(1, owners)
    def _(step):
        other = lax.rem(me + step, owners)
        pl.semaphore_signal(barrier, inc=1, device_id={"grp": other}, device_id_type=MESH)

    loads = []
    for t in range(tiles):
        load = pltpu.make_async_copy(
            starter_ref.at[:, :, t * LANES : (t + 1) * LANES], start.at[t], start_sem.at[t]
        )
        load.start()
        loads.append(load)
    load_csm = pltpu.make_async_copy(csm_ref, csm, local_sem.at[1])
    load_weight = pltpu.make_async_copy(weight_ref, weight, local_sem.at[2])

    def spread(ref, r):
        return jnp.broadcast_to(ref[r : r + 1, :], (hydros, cols)) - 2.0

    def place_rows(which):
        for t in range(tiles):
            for part in range(2):
                for r in which:
                    field[part, RIM + r, :, t * LANES : (t + 1) * LANES] = start[
                        t, part, pl.ds(r, hydros, stride=rows), :
                    ]

    for load in loads:
        load.wait()
    place_rows([*range(RIM), *range(rows - RIM, rows)])

    col = lax.broadcasted_iota(jnp.int32, (hydros, cols), 1)

    def operate(ref, part, r, half):
        here = ref[part, r]
        left = jnp.where(col == 0, 0.0, pltpu.roll(here, 1, 1))
        right = jnp.where(col == cols - 1, 0.0, pltpu.roll(here, cols - 1, 1))
        total = (ref[part, r - 1] + ref[part, r + 1]) + (left + right)
        return half * total + coef[r] * here

    def scale(r):
        if not isinstance(r, int) or RIM <= r < RIM + rows:
            return 0.5
        outside = slab == (0 if r < RIM else slabs - 1)
        return jnp.where(outside, 0.0, 0.5).astype(jnp.float32)

    def apply_first(source, r):
        half = scale(r)
        for part in range(2):
            first[part, r] = operate(source, part, r, half)

    def advance(source, r):
        half = scale(r)
        fr, fi = first[0, r], first[1, r]
        sr = operate(first, 0, r, half)
        si = operate(first, 1, r, half)
        real = source[0, r] - first_imag * fi + second_coef[0] * sr - second_coef[1] * si
        imag = source[1, r] + first_imag * fr + second_coef[1] * sr + second_coef[0] * si
        return real, imag

    def first_one(r):
        apply_first(field, r)

    def step_one(r):
        real, imag = advance(field, r)
        middle[0, r] = real
        middle[1, r] = imag

    def first_two(r):
        apply_first(middle, r)

    def step_two(block, base, r):
        real, imag = advance(middle, r)
        for t in range(tiles):
            owner = (r - base) * tiles + t
            outgoing[block, owner, 0] = real[:, t * LANES : (t + 1) * LANES]
            outgoing[block, owner, 1] = imag[:, t * LANES : (t + 1) * LANES]

    pl.semaphore_wait(barrier, owners + 1)

    def rim_copy(k, source, target, other):
        return pltpu.make_async_remote_copy(
            src_ref=source, dst_ref=target, send_sem=rim_send.at[k], recv_sem=rim_recv.at[k],
            device_id={"row": other}, device_id_type=MESH,
        )

    rims = [
        rim_copy(0, field.at[:, pl.ds(RIM, RIM)], field.at[:, pl.ds(RIM + rows, RIM)], above),
        rim_copy(1, field.at[:, pl.ds(rows, RIM)], field.at[:, pl.ds(0, RIM)], below),
        rim_copy(2, medium_ref.at[pl.ds(0, 8)], medium_below, above),
        rim_copy(3, medium_ref.at[pl.ds(rows - 8, 8)], medium_above, below),
    ]
    for copy in rims:
        copy.start()

    def block_copy(block, source, target):
        return pltpu.make_async_remote_copy(
            src_ref=outgoing.at[block, target], dst_ref=vectors.at[block, source],
            send_sem=block_send.at[block, target], recv_sem=block_recv.at[block, source],
            device_id={"grp": target}, device_id_type=MESH,
        )

    def send_blocks(block):
        @pl.loop(1, owners)
        def _(step):
            block_copy(block, me, farthest_first(step)).start()

        own = pltpu.make_async_copy(
            outgoing.at[block, me], vectors.at[block, me], local_sem.at[3 + block]
        )
        own.start()
        return own

    load_csm.start()
    load_weight.start()
    place_rows(range(RIM, rows - RIM))
    for r in range(rows):
        coef[RIM + r] = spread(medium_ref, r)

    def pairs(low, high, body):
        def both(i, carry):
            body(low + 2 * i)
            body(low + 2 * i + 1)
            return carry

        lax.fori_loop(0, (high - low) // 2, both, 0)

    pairs(RIM + 1, RIM + rows - 1, first_one)
    pairs(RIM + 2, RIM + rows - 2, step_one)
    pairs(RIM + 3, RIM + rows - 3, first_two)
    pairs(RIM + 4, RIM + rows - 4, functools.partial(step_two, 0, RIM + 4))

    own_inner = send_blocks(0)

    for copy in rims:
        copy.wait_recv()

    @pl.when(slab == 0)
    def _():
        field[:, 0:RIM] = jnp.zeros((2, RIM, hydros, cols), jnp.float32)

    @pl.when(slab == slabs - 1)
    def _():
        field[:, RIM + rows :] = jnp.zeros((2, RIM, hydros, cols), jnp.float32)

    for r in range(RIM):
        coef[r] = spread(medium_above, 8 - RIM + r)
        coef[RIM + rows + r] = spread(medium_below, r)

    top = RIM + rows
    for stage, body in enumerate((first_one, step_one, first_two)):
        for r in range(RIM):
            body(1 + stage + r)
            body(top - 1 - stage + r)
    for r in range(RIM):
        step_two(1, RIM, RIM + r)
        step_two(1, RIM + inner, top - RIM + r)

    own_outer = send_blocks(1)

    load_csm.wait()
    load_weight.wait()
    own_inner.wait()
    own_outer.wait()

    def dot(a, b):
        return jnp.dot(a, b, precision=lax.Precision.HIGHEST, preferred_element_type=jnp.float32)

    for block in range(2):
        @pl.loop(1, owners)
        def _(step):
            block_copy(block, lax.rem(me + step, owners), me).wait_recv()

        u, v = (vectors[block, :, part].reshape(owners * hydros, LANES) for part in range(2))
        both = jnp.concatenate([u, v], axis=1)

        def form(matrix):
            near = dot(matrix[0], both)
            cross = dot(matrix[1], u)
            return jnp.sum(
                u * near[:, :LANES] + v * (near[:, LANES:] + 2.0 * cross), axis=0, keepdims=True
            )

        power = jnp.sum(u * u + v * v, axis=0, keepdims=True) + 1e-06
        mine[block : block + 1] = form(csm) / power
        mine[2 + block : 3 + block] = power / form(weight)

    def result_copy(source, target):
        return pltpu.make_async_remote_copy(
            src_ref=mine, dst_ref=table.at[source],
            send_sem=result_send.at[target], recv_sem=result_recv.at[source],
            device_id={"grp": target}, device_id_type=MESH,
        )

    @pl.loop(1, owners)
    def _(step):
        result_copy(me, farthest_first(step)).start()

    own_result = pltpu.make_async_copy(mine, table.at[me], local_sem.at[5])
    own_result.start()

    share = result_ref.shape[1]
    wanted = cells_ref[:, pl.ds(pl.multiple_of(me * share, share), share)]
    tile = wanted // LANES
    lane = wanted - tile * LANES
    edge = (inner // 2) * tiles
    is_inner = (tile >= edge) & (tile < edge + owners)
    owner = jnp.where(is_inner, tile - edge, jnp.where(tile < edge, tile, tile - owners))
    entry = owner * 4 + jnp.where(is_inner, 0, 1)
    place = lax.broadcasted_iota(jnp.int32, (owners * 4, share), 0)
    pick_bartlett = jnp.where(place == entry, 1.0, 0.0)
    pick_capon = jnp.where(place == entry + 2, 1.0, 0.0)
    on_lane = lax.broadcasted_iota(jnp.int32, (LANES, share), 0) == lane

    own_result.wait()

    @pl.loop(1, owners)
    def _(step):
        result_copy(lax.rem(me + step, owners), me).wait_recv()

    flat = table[...].reshape(owners * 4, LANES).T

    def take(pick):
        chosen = jnp.dot(
            flat, pick, precision=lax.Precision.HIGHEST, preferred_element_type=jnp.float32
        )
        return jnp.sum(jnp.where(on_lane, chosen, 0.0), axis=0, keepdims=True)

    result_ref[0:1] = take(pick_bartlett)
    result_ref[1:2] = take(pick_capon)

    for copy in rims:
        copy.wait_send()

    @pl.loop(1, owners)
    def _(step):
        other = lax.rem(me + step, owners)
        block_copy(0, me, other).wait_send()
        block_copy(1, me, other).wait_send()
        result_copy(me, other).wait_send()


def on_device(starter, medium, csm, capon_weight, search_cells):
    parts, hydros, rows, cols = starter.shape
    owners = lax.axis_size("grp")
    slabs = lax.axis_size("row")
    depth = rows + 2 * RIM
    share = search_cells.shape[1] // owners
    vmem = pl.BlockSpec(memory_space=pltpu.VMEM)
    anywhere = pl.BlockSpec(memory_space=pl.ANY)
    plane = pltpu.VMEM((parts, depth, hydros, cols), jnp.float32)
    blocks = pltpu.VMEM((2, owners, parts, hydros, LANES), jnp.float32)
    result = pl.pallas_call(
        functools.partial(kernel, owners, slabs, rows),
        out_shape=jax.ShapeDtypeStruct((2, share), jnp.float32),
        in_specs=[anywhere, vmem, anywhere, anywhere, vmem],
        out_specs=vmem,
        scratch_shapes=[
            pltpu.VMEM((cols // LANES, parts, hydros * rows, LANES), jnp.float32),
            plane,
            plane,
            plane,
            pltpu.VMEM((depth, hydros, cols), jnp.float32),
            pltpu.VMEM((8, cols), jnp.float32),
            pltpu.VMEM((8, cols), jnp.float32),
            blocks,
            blocks,
            pltpu.VMEM(csm.shape, jnp.float32),
            pltpu.VMEM(csm.shape, jnp.float32),
            pltpu.VMEM((4, LANES), jnp.float32),
            pltpu.VMEM((owners, 4, LANES), jnp.float32),
            pltpu.SemaphoreType.DMA((cols // LANES,)),
            pltpu.SemaphoreType.DMA((6,)),
            pltpu.SemaphoreType.DMA((4,)),
            pltpu.SemaphoreType.DMA((4,)),
            pltpu.SemaphoreType.DMA((2, owners)),
            pltpu.SemaphoreType.DMA((2, owners)),
            pltpu.SemaphoreType.DMA((owners,)),
            pltpu.SemaphoreType.DMA((owners,)),
        ],
        compiler_params=pltpu.CompilerParams(collective_id=0, has_side_effects=True),
    )(starter.reshape(parts, hydros * rows, cols), medium, csm, capon_weight, search_cells)
    return result[0:1], result[1:2]


def solution(mesh):
    return jax.shard_map(
        on_device,
        mesh=mesh,
        in_specs=(P(None, "grp", "row", None), P("row", None), P(), P(), P("row", None)),
        out_specs=(P("row", "grp"), P("row", "grp")),
        check_vma=False,
    )
```
